128 devices in a mesh: dp: 16 (over z, x), tensor: 8 (over y, core).
Axes of the slice: x: 4, y: 4, z: 4, core: 2. Of those that a mesh axis runs over, the one named last changes fastest.
Arguments:
- inputs: bfloat16 [6144, 12288], P('dp', 'tensor'), may hold values from -160 to 160
- out_grad: bfloat16 [6144, 6144], P('dp'), may hold values from -0.08930431 to 0.08930431
- weight_codes: bfloat16 [6144, 12288], P('dp', 'tensor'), may hold values from -1 to 1
- weight_scales: bfloat16 [6144], P('dp'), may hold values from 0.0039978027 to 0.019897461
- master: float32 [6144, 12288], P('dp', 'tensor'), may hold values from -0.8 to 0.8
- moment: float32 [6144, 12288], P('dp', 'tensor'), may hold values from -3 to 3
- second: float32 [6144, 12288], P('dp', 'tensor'), may hold values from 0.05 to 0.5
Outputs:
- grad_input: bfloat16 [6144, 12288], P('dp', 'tensor')
- new_master: float32 [6144, 12288], P('dp', 'tensor')
- new_moment: float32 [6144, 12288], P('dp', 'tensor')
- new_second: float32 [6144, 12288], P('dp', 'tensor')
- new_codes: bfloat16 [6144, 12288], P('dp', 'tensor')
- new_scales: bfloat16 [6144], P('dp')
- grad_peak: float32 [], replicated
The draws below stay inside these ranges and needn't reach their ends.
All inputs are finite; a program needn't handle non-finite values. Where the reference program divides by a largest or mean magnitude, that divisor is 1e-20 or more.
Results may differ from the reference program's by a relative error of at most 0.019.
Values may be sent and summed in bfloat16 or wider, within the bound.
No kernel may reach another device: no remote copies, remote signals or barrier semaphores. Data moves between devices by JAX's collectives and lax.ppermute only.
A program may use at most 192 MiB of HBM per device.

```python
import math
import jax
import jax.numpy as jnp
from jax import lax

IN = 12288
OUT = 6144
TOK_DEV = 384
TOKENS = 6144
N_DP = 16


def rising(number):
    return jnp.power(3.0, jnp.arange(number, dtype=jnp.float32) / max(number - 1, 1))


def scaled_field(key, height, width, spread):
    normal_key = jax.random.fold_in(jax.random.fold_in(key, 11), 0)
    row_scale = rising(height)
    column_scale = rising(width)
    base = jnp.clip(jax.random.normal(normal_key, (height, width), jnp.float32), -4.0, 4.0)
    return spread * base * row_scale[:, None] * column_scale[None, :]


def draw_inputs(key, part):
    return scaled_field(key, TOKENS, IN, 1.0).astype(jnp.bfloat16)


def draw_out_grad(key, part):
    spread = 0.045 / TOKENS ** 0.5
    return scaled_field(jax.random.fold_in(key, 5), TOKENS, OUT, spread).astype(jnp.bfloat16)


def draw_master(key, part):
    normal_key = jax.random.fold_in(jax.random.fold_in(key, 7), 0)
    column_scale = rising(IN)
    base = jnp.clip(jax.random.normal(normal_key, (OUT, IN), jnp.float32), -4.0, 4.0)
    return 0.02 * base * column_scale[None, :]


def level_of(stream_key, shape, cuts, least, largest):
    factor_of = 1.0
    for dim, parts in cuts:
        steps = jax.random.uniform(jax.random.fold_in(jax.random.fold_in(stream_key, 6), dim), (parts,), jnp.float32, least / len(cuts), largest / len(cuts))
        factor_of = factor_of * jnp.repeat(jnp.exp(steps), shape[dim] // parts).reshape((-1,) + (1,) * (len(shape) - 1 - dim))
    return factor_of


def noise(key, dims, deviation, reach, cuts=(), kind=jnp.bfloat16):
    drawn = deviation * jax.random.normal(key, dims, jnp.float32)
    if cuts:
        drawn = drawn * level_of(key, dims, cuts, -0.22, 0.18)
    return jnp.clip(drawn, -reach, reach).astype(kind)


def setup_inputs(seed: int = 0) -> dict:
    arg_keys = jax.random.split(jax.random.key(seed), 8)
    return {
        "inputs": draw_inputs(jax.random.fold_in(arg_keys[7], 71), 0),
        "out_grad": draw_out_grad(jax.random.fold_in(arg_keys[7], 71), 0),
        "weight_codes": jnp.clip(jax.random.uniform(arg_keys[2], (OUT, IN), jnp.float32, -1.0, 1.0) * level_of(arg_keys[2], (OUT, IN), ((0, 16), (1, 8)), -0.4, 0.0), -1.0, 1.0).astype(jnp.bfloat16),
        "weight_scales": jnp.clip(jnp.exp(math.log(0.019897461) - 1.6048472 * jax.random.uniform(arg_keys[3], (OUT,), jnp.float32) ** level_of(arg_keys[3], (OUT,), ((0, 16),), -0.2, 0.2)), 0.0039978027, 0.019897461).astype(jnp.bfloat16),
        "master": draw_master(jax.random.fold_in(arg_keys[7], 71), 0),
        "moment": noise(arg_keys[5], (OUT, IN), 0.5, 3.0, ((0, 16), (1, 8)), jnp.float32),
        "second": jnp.clip(jnp.exp(math.log(0.5) - 2.3025851 * jax.random.uniform(arg_keys[6], (OUT, IN), jnp.float32) ** level_of(arg_keys[6], (OUT, IN), ((0, 16), (1, 8)), -0.2, 0.2)), 0.05, 0.5),
    }


def block_term(grads, acts):
    return lax.dot_general(grads, acts, (((0,), (0,)), ((), ())), preferred_element_type=jnp.float32)

def grid_round(partial_value, divisor):
    scaled = lax.optimization_barrier((partial_value / divisor * 64.0).astype(jnp.bfloat16))
    return scaled.astype(jnp.float32)

def reference(inputs, out_grad, weight_codes, weight_scales, master, moment, second):
    weight = (weight_codes.astype(jnp.float32) * weight_scales.astype(jnp.float32)[:, None]).astype(jnp.bfloat16)
    grad_input = jnp.dot(out_grad, weight, preferred_element_type=jnp.float32).astype(jnp.bfloat16)
    acts_blocks = inputs.reshape(N_DP, TOK_DEV, IN)
    grad_blocks = out_grad.reshape(N_DP, TOK_DEV, OUT)

    def peak_step(carry, pair):
        return (jnp.maximum(carry, jnp.max(jnp.abs(block_term(pair[0], pair[1])))), None)
    grad_peak = lax.scan(peak_step, jnp.zeros((), jnp.float32), (grad_blocks, acts_blocks))[0]
    divisor = grad_peak + 1e-06

    def sum_step(carry, pair):
        return (carry + grid_round(block_term(pair[0], pair[1]), divisor), None)
    summed = lax.scan(sum_step, jnp.zeros((OUT, IN), jnp.float32), (grad_blocks, acts_blocks))[0]
    gradient = summed * divisor / 64.0
    total_norm = jnp.sqrt(jnp.sum(gradient * gradient))
    clip_factor = jnp.minimum(1.0, jnp.sqrt(jnp.float32(OUT * IN)) / (total_norm + 1e-06))
    clipped = clip_factor * gradient
    new_moment = 0.9 * moment + 0.1 * clipped
    new_second = 0.95 * second + 0.05 * clipped * clipped
    new_master = master - 0.01 * (new_moment / (jnp.sqrt(new_second) + 1e-08) + 0.1 * master)
    row_peak = lax.optimization_barrier(jnp.max(jnp.abs(new_master), axis=1)) + 1e-06
    new_codes = (new_master / row_peak[:, None]).astype(jnp.bfloat16)
    new_scales = row_peak.astype(jnp.bfloat16)
    return (grad_input, new_master, new_moment, new_second, new_codes, new_scales, grad_peak)
```

```python
import functools
import jax
import jax.numpy as jnp
from jax import lax
from jax.experimental import pallas as pl
from jax.experimental.pallas import tpu as pltpu
from jax.sharding import Mesh
from jax.sharding import PartitionSpec as P

ALL = ("z", "x", "y", "c")
DP = ("z", "x")
TENSOR = ("y", "c")
IN = 12288
OUT = 6144
S = 384
C = 1536
HALF = S // 2
SUB = S // 8
NT = 256
BF = jnp.bfloat16
F32 = jnp.float32
RZ = (2, 1, 3, 0)


def shift(v, axis, by):
    n = 4 if axis != "c" else 2
    return lax.ppermute(v, axis, [(i, (i + by) % n) for i in range(n)])


def params(mib):
    return pltpu.CompilerParams(vmem_limit_bytes=mib << 20)


def vmem():
    return pl.BlockSpec(memory_space=pltpu.VMEM)


def split_kernel(at, grad_ref, *outs):
    z, x = at[1], at[2]
    for out, rx in zip(outs, (1, 3, 2)):
        for k, rz in enumerate(RZ):
            block = lax.rem(z + rz, 4) * 4 + lax.rem(x + rx, 4)
            out[:, k * S : (k + 1) * S] = grad_ref[:, pl.ds(pl.multiple_of(block * S, S), S)]


def split_grads(at, out_grad):
    piece = jax.ShapeDtypeStruct((SUB, C), BF)
    whole = pl.BlockSpec((SUB, C), lambda i, at: (0, 0))
    return pl.pallas_call(
        split_kernel,
        grid_spec=pltpu.PrefetchScalarGridSpec(
            num_scalar_prefetch=1,
            grid=(1,),
            in_specs=[pl.BlockSpec((SUB, OUT), lambda i, at: (at[0], 0))],
            out_specs=[whole] * 3,
        ),
        out_shape=[piece] * 3,
        name="split_grads",
    )(at, out_grad)


def assemble_kernel(at, *refs):
    own, chunks, (rows_ref, cols_ref) = refs[:4], refs[4:12], refs[12:]
    y, c = at[3], at[4]
    for k in range(4):
        rows_ref[0, :, k * S : (k + 1) * S] = own[k][...]
    for core in range(2):
        for i, ry in enumerate((0, 3, 1, 2)):
            source = lax.rem(y + ry, 4) * 2 + lax.rem(c + core, 2)
            top = pl.multiple_of(source * SUB, SUB)
            for j in range(3):
                rows_ref[1 + j, pl.ds(top, SUB), :] = chunks[core * 4 + i][j * SUB : (j + 1) * SUB, :]
    for j in range(4):
        for k in range(4):
            cols_ref[k, :, j * S : (j + 1) * S] = rows_ref[j, :, k * S : (k + 1) * S].T


def assemble(at, out_grad, chunks):
    def own(rz):
        return pl.BlockSpec(
            (S, S), lambda i, at: (0, lax.rem(at[1] + rz, 4) * 4 + at[2])
        )

    full = pl.BlockSpec((3 * SUB, C), lambda i, at: (0, 0))
    out = pl.BlockSpec((4, S, C), lambda i, at: (0, 0, 0))
    return pl.pallas_call(
        assemble_kernel,
        grid_spec=pltpu.PrefetchScalarGridSpec(
            num_scalar_prefetch=1,
            grid=(1,),
            in_specs=[own(rz) for rz in RZ] + [full] * 8,
            out_specs=[out, out],
        ),
        out_shape=[jax.ShapeDtypeStruct((4, S, C), BF)] * 2,
        compiler_params=params(40),
        name="assemble_grads",
    )(at, *([out_grad] * 4), *chunks)


def weight_grad_kernel(count, own_last, *refs):
    cols, acts, outs = refs[:count], refs[count : count + 5], refs[count + 5 :]
    peak_ref, outs = outs[-1], outs[:-1]
    peak_ref[...] = jnp.zeros_like(peak_ref)

    def step(i, carry):
        at = pl.ds(pl.multiple_of(i * NT, NT), NT)
        a, b, d, e, f = acts
        right = [a[:, at], b[:, at], d[:, at], jnp.concatenate([e[:, at], f[:, at]], axis=0)]
        peak = peak_ref[...]
        for k in range(count):
            total = None
            for j in range(4):
                part = jnp.dot(
                    cols[k][0, :, j * S : (j + 1) * S], right[j], preferred_element_type=F32
                )
                high = jnp.max(jnp.abs(part).reshape(S // 8, 8, NT), axis=0)
                peak = jnp.maximum(peak, high)
                total = part if total is None else total + part
            if own_last:
                outs[k][:, at] = total
            else:
                outs[2 * k][:, at] = total[:HALF].astype(BF)
                outs[2 * k + 1][:, at] = total[HALF:].astype(BF)
        peak_ref[...] = peak
        return carry

    lax.fori_loop(0, C // NT, step, 0)


def weight_grad(cols, blocks, acts, own):
    half = jax.ShapeDtypeStruct((HALF, C), BF)
    outs = [jax.ShapeDtypeStruct((S, C), F32)] if own else [half] * (2 * len(blocks))
    outs = outs + [jax.ShapeDtypeStruct((8, NT), F32)]

    def piece(k):
        return pl.BlockSpec((1, S, C), lambda i: (k, 0, 0))

    def whole(v):
        return pl.BlockSpec(v.shape, lambda i: (0, 0))

    return pl.pallas_call(
        functools.partial(weight_grad_kernel, len(blocks), own),
        grid=(1,),
        in_specs=[piece(k) for k in blocks] + [whole(v) for v in acts],
        out_specs=[whole(v) for v in outs],
        out_shape=outs,
        compiler_params=params(40),
        cost_estimate=pl.CostEstimate(
            flops=2 * len(blocks) * S * C * C, bytes_accessed=9 << 20, transcendentals=0
        ),
        name="weight_grad",
    )(*([cols] * len(blocks)), *acts)


def input_grad_kernel(count, own_last, *refs):
    rows, weights, outs = refs[:count], refs[count : count + 5], refs[count + 5 :]

    def step(i, carry):
        at = pl.ds(pl.multiple_of(i * NT, NT), NT)
        right = jnp.concatenate([w[:, at] for w in weights], axis=0)
        for k in range(count):
            total = jnp.dot(rows[k][0], right, preferred_element_type=F32)
            if own_last:
                outs[k][:, at] = total
            else:
                outs[2 * k][:, at] = total[:HALF].astype(BF)
                outs[2 * k + 1][:, at] = total[HALF:].astype(BF)
        return carry

    lax.fori_loop(0, C // NT, step, 0)


def input_grad(rows, blocks, weights, own):
    half = jax.ShapeDtypeStruct((HALF, C), BF)
    outs = [jax.ShapeDtypeStruct((S, C), F32)] if own else [half] * (2 * len(blocks))

    def piece(k):
        return pl.BlockSpec((1, S, C), lambda i: (k, 0, 0))

    def whole(v):
        return pl.BlockSpec(v.shape, lambda i: (0, 0))

    return pl.pallas_call(
        functools.partial(input_grad_kernel, len(blocks), own),
        grid=(1,),
        in_specs=[piece(k) for k in blocks] + [whole(v) for v in weights],
        out_specs=[whole(v) for v in outs],
        out_shape=outs,
        compiler_params=params(40),
        cost_estimate=pl.CostEstimate(
            flops=2 * len(blocks) * S * C * C, bytes_accessed=9 << 20, transcendentals=0
        ),
        name="input_grad",
    )(*([rows] * len(blocks)), *weights)


def ring_gather(v, axis):
    left = shift(v, axis, 1)
    right = shift(v, axis, -1)
    top = shift(left[:HALF], axis, 1)
    bottom = shift(right[HALF:], axis, -1)
    return v, left, right, top, bottom


def ring_scatter(far, near, own, axis):
    up_a, up_b, down_a, down_b = near
    from_left = shift(far[0], axis, 1)
    from_right = shift(far[1], axis, -1)
    left_b = shift(up_b, axis, 1)
    right_a = shift(down_a, axis, -1)
    left_a = shift((up_a.astype(F32) + from_left.astype(F32)).astype(BF), axis, 1)
    right_b = shift((down_b.astype(F32) + from_right.astype(F32)).astype(BF), axis, -1)
    top = own[:HALF] + left_a.astype(F32) + right_a.astype(F32)
    bottom = own[HALF:] + left_b.astype(F32) + right_b.astype(F32)
    return jnp.concatenate([top, bottom], axis=0)


def on_device(inputs, out_grad, weight_codes, weight_scales, master, moment, second):
    z, x, y, c = (lax.axis_index(a) for a in ALL)
    at = jnp.stack([y * 2 + c, z, x, y, c]).astype(jnp.int32)

    to_up, to_down, to_far = split_grads(at, out_grad)
    mine = jnp.concatenate(
        [shift(to_up, "x", 1), shift(to_down, "x", -1), shift(to_far, "x", 2)], axis=0
    )
    acts = ring_gather(inputs, "x")
    held = [mine] + [shift(mine, "y", s) for s in (1, -1, 2)]
    other = [shift(v, "c", 1) for v in held]
    rows, cols = assemble(at, out_grad, held + other)

    weight = (weight_codes.astype(F32) * weight_scales.astype(F32)[:, None]).astype(BF)
    w_own, w_left, w_right, w_top, w_bottom = ring_gather(weight, "z")
    weights = (w_top, w_bottom, w_right, w_left, w_own)

    far = weight_grad(cols, (0,), acts, False)
    near = weight_grad(cols, (1, 2), acts, False)
    own = weight_grad(cols, (3,), acts, True)
    local_peak = jnp.maximum(jnp.maximum(far[-1], near[-1]), own[-1]).max()
    gradient = ring_scatter(far[:2], near[:4], own[0], "z")

    i_far = input_grad(rows, (3,), weights, False)
    i_near = input_grad(rows, (2, 1), weights, False)
    i_own = input_grad(rows, (0,), weights, True)
    grad_input = ring_scatter(i_far, i_near, i_own[0], "x").astype(BF)

    pair = jnp.stack([jnp.sum(gradient * gradient), local_peak])
    pairs = lax.all_to_all(jnp.broadcast_to(pair[None], (128, 2)), ALL, 0, 0, tiled=True)
    squares = jnp.sum(pairs[:, 0])
    grad_peak = jnp.max(pairs[:, 1])

    clip_factor = jnp.minimum(1.0, jnp.sqrt(F32(OUT * IN)) / (jnp.sqrt(squares) + 1e-06))
    clipped = clip_factor * gradient
    new_moment = 0.9 * moment + 0.1 * clipped
    new_second = 0.95 * second + 0.05 * clipped * clipped
    new_master = master - 0.01 * (new_moment / (jnp.sqrt(new_second) + 1e-08) + 0.1 * master)
    high = jnp.max(jnp.abs(new_master), axis=1)
    highs = lax.all_to_all(jnp.broadcast_to(high[None], (8, S)), TENSOR, 0, 0, tiled=True)
    row_peak = highs.max(axis=0) + 1e-06
    new_codes = (new_master / row_peak[:, None]).astype(BF)
    new_scales = row_peak.astype(BF)
    return (grad_input, new_master, new_moment, new_second, new_codes, new_scales, grad_peak)


def solution(mesh):
    finer = Mesh(mesh.devices.reshape(4, 4, 4, 2), ALL)
    tiled = P(DP, TENSOR)
    in_specs = (tiled, P(DP, None), tiled, P(DP), tiled, tiled, tiled)
    out_specs = (tiled, tiled, tiled, tiled, tiled, P(DP), P())
    return jax.shard_map(
        on_device, mesh=finer, in_specs=in_specs, out_specs=out_specs, check_vma=False
    )
```

```python
import functools
import jax
import jax.numpy as jnp
from jax import lax
from jax.experimental import pallas as pl
from jax.experimental.pallas import tpu as pltpu
from jax.sharding import Mesh
from jax.sharding import PartitionSpec as P

ALL = ("z", "x", "y", "c")
DP = ("z", "x")
TENSOR = ("y", "c")
IN = 12288
OUT = 6144
S = 384
C = 1536
HALF = S // 2
SUB = S // 8
NT = 256
BF = jnp.bfloat16
F32 = jnp.float32
RZ = (2, 1, 3, 0)


def shift(v, axis, by):
    n = 4 if axis != "c" else 2
    return lax.ppermute(v, axis, [(i, (i + by) % n) for i in range(n)])


def params(mib):
    return pltpu.CompilerParams(vmem_limit_bytes=mib << 20)


def split_kernel(grad_ref, *refs):
    outs, slab, sem = refs[:3], refs[3], refs[4]
    z, x, y, c = (lax.axis_index(a) for a in ALL)
    top = pl.multiple_of((y * 2 + c) * SUB, SUB)
    copy = pltpu.make_async_copy(grad_ref.at[pl.ds(top, SUB), :], slab, sem)
    copy.start()
    copy.wait()
    for out, rx in zip(outs, (1, 3, 2)):
        for k, rz in enumerate(RZ):
            block = lax.rem(z + rz, 4) * 4 + lax.rem(x + rx, 4)
            out[:, k * S : (k + 1) * S] = slab[:, pl.ds(pl.multiple_of(block * S, S), S)]


def split_grads(out_grad):
    piece = jax.ShapeDtypeStruct((SUB, C), BF)
    return pl.pallas_call(
        split_kernel,
        in_specs=[pl.BlockSpec(memory_space=pltpu.HBM)],
        out_specs=[pl.BlockSpec(memory_space=pltpu.VMEM)] * 3,
        out_shape=[piece] * 3,
        scratch_shapes=[pltpu.VMEM((SUB, OUT), BF), pltpu.SemaphoreType.DMA],
        compiler_params=params(8),
        name="split_grads",
    )(out_grad)


def assemble_kernel(*refs):
    grad_ref, chunks, (rows_ref, cols_ref) = refs[0], refs[1:9], refs[9:]
    z, x, y, c = (lax.axis_index(a) for a in ALL)
    for k, rz in enumerate(RZ):
        block = lax.rem(z + rz, 4) * 4 + x
        rows_ref[0, :, k * S : (k + 1) * S] = grad_ref[:, pl.ds(pl.multiple_of(block * S, S), S)]
    for core in range(2):
        for i, ry in enumerate((0, 3, 1, 2)):
            source = lax.rem(y + ry, 4) * 2 + lax.rem(c + core, 2)
            top = pl.multiple_of(source * SUB, SUB)
            for j in range(3):
                rows_ref[1 + j, pl.ds(top, SUB), :] = chunks[core * 4 + i][
                    j * SUB : (j + 1) * SUB, :
                ]
    for j in range(4):
        for k in range(4):
            cols_ref[k, :, j * S : (j + 1) * S] = rows_ref[j, :, k * S : (k + 1) * S].T


def assemble(out_grad, chunks):
    full = pl.BlockSpec((3 * SUB, C), lambda i: (0, 0))
    out = pl.BlockSpec((4, S, C), lambda i: (0, 0, 0))
    return pl.pallas_call(
        assemble_kernel,
        grid=(1,),
        in_specs=[pl.BlockSpec((S, OUT), lambda i: (0, 0))] + [full] * 8,
        out_specs=[out, out],
        out_shape=[jax.ShapeDtypeStruct((4, S, C), BF)] * 2,
        compiler_params=params(28),
        name="assemble_grads",
    )(out_grad, *chunks)


def weight_grad_kernel(blocks, width, *refs):
    count = len(blocks)
    cols, acts, outs = refs[:count], refs[count : count + 5], refs[count + 5 :]
    peak_ref = outs[-1]
    peak_ref[...] = jnp.zeros_like(peak_ref)

    def step(i, carry):
        at = pl.ds(pl.multiple_of(i * NT, NT), NT)
        right = [acts[j][:, at] for j in range(3)]
        right.append(jnp.concatenate([acts[3][:, at], acts[4][:, at]], axis=0))
        peak = peak_ref[...]
        n = 0
        for k, block in enumerate(blocks):
            total = None
            for j in range(4):
                part = jnp.dot(
                    cols[k][0, :, j * S : (j + 1) * S], right[j], preferred_element_type=F32
                )
                high = jnp.max(jnp.abs(part).reshape(S // 8, 8, NT), axis=0)
                peak = jnp.maximum(peak, high)
                total = part if total is None else total + part
            if block == 3:
                outs[n][:, at] = total
                n += 1
            else:
                outs[n][:, at] = total[:HALF].astype(BF)
                outs[n + 1][:, at] = total[HALF:].astype(BF)
                n += 2
        peak_ref[...] = peak
        return carry

    lax.fori_loop(0, width // NT, step, 0)


def weight_grad(cols, blocks, acts):
    width = acts[0].shape[1]
    outs = []
    for block in blocks:
        if block == 3:
            outs.append(jax.ShapeDtypeStruct((S, width), F32))
        else:
            outs += [jax.ShapeDtypeStruct((HALF, width), BF)] * 2
    outs.append(jax.ShapeDtypeStruct((8, NT), F32))

    def piece(k):
        return pl.BlockSpec((1, S, C), lambda i: (k, 0, 0))

    def whole(v):
        return pl.BlockSpec(v.shape, lambda i: (0, 0))

    return pl.pallas_call(
        functools.partial(weight_grad_kernel, blocks, width),
        grid=(1,),
        in_specs=[piece(k) for k in blocks] + [whole(v) for v in acts],
        out_specs=[whole(v) for v in outs],
        out_shape=outs,
        compiler_params=params(24),
        cost_estimate=pl.CostEstimate(
            flops=2 * len(blocks) * S * C * width, bytes_accessed=9 << 20, transcendentals=0
        ),
        name="weight_grad",
    )(*([cols] * len(blocks)), *acts)


def far_start_kernel(cols_ref, own_ref, left_ref, right_ref, part_ref, peak_ref):
    peak_ref[...] = jnp.zeros_like(peak_ref)

    def step(i, carry):
        at = pl.ds(pl.multiple_of(i * NT, NT), NT)
        peak, total = peak_ref[...], None
        for j, ref in enumerate((own_ref, left_ref, right_ref)):
            part = jnp.dot(
                cols_ref[0, :, j * S : (j + 1) * S], ref[:, at], preferred_element_type=F32
            )
            peak = jnp.maximum(peak, jnp.max(jnp.abs(part).reshape(S // 8, 8, NT), axis=0))
            total = part if total is None else total + part
        part_ref[:, at] = total
        peak_ref[...] = peak
        return carry

    lax.fori_loop(0, C // NT, step, 0)


def far_finish_kernel(cols_ref, part_ref, top_ref, low_ref, peak_in, high_ref, low_out, peak_ref):
    peak_ref[...] = peak_in[...]

    def step(i, carry):
        at = pl.ds(pl.multiple_of(i * NT, NT), NT)
        right = jnp.concatenate([top_ref[:, at], low_ref[:, at]], axis=0)
        part = jnp.dot(cols_ref[0], right, preferred_element_type=F32)
        high = jnp.max(jnp.abs(part).reshape(S // 8, 8, NT), axis=0)
        peak_ref[...] = jnp.maximum(peak_ref[...], high)
        total = part_ref[:, at] + part
        high_ref[:, at] = total[:HALF].astype(BF)
        low_out[:, at] = total[HALF:].astype(BF)
        return carry

    lax.fori_loop(0, C // NT, step, 0)


def whole(shape):
    return pl.BlockSpec(shape, lambda i: (0,) * len(shape))


def weight_grad_far(cols, acts):
    small = jax.ShapeDtypeStruct((8, NT), F32)
    half = jax.ShapeDtypeStruct((HALF, C), BF)
    part, peak = pl.pallas_call(
        far_start_kernel,
        grid=(1,),
        in_specs=[whole((1, S, C))] + [whole((S, C))] * 3,
        out_specs=[whole((S, C)), whole((8, NT))],
        out_shape=[jax.ShapeDtypeStruct((S, C), F32), small],
        compiler_params=params(24),
        cost_estimate=pl.CostEstimate(
            flops=6 * S * S * C, bytes_accessed=6 << 20, transcendentals=0
        ),
        name="far_start",
    )(cols, *acts[:3])
    return pl.pallas_call(
        far_finish_kernel,
        grid=(1,),
        in_specs=[
            pl.BlockSpec((1, S, S), lambda i: (0, 0, 3)),
            whole((S, C)),
            whole((HALF, C)),
            whole((HALF, C)),
            whole((8, NT)),
        ],
        out_specs=[whole((HALF, C)), whole((HALF, C)), whole((8, NT))],
        out_shape=[half, half, small],
        compiler_params=params(24),
        cost_estimate=pl.CostEstimate(
            flops=2 * S * S * C, bytes_accessed=4 << 20, transcendentals=0
        ),
        name="far_finish",
    )(cols, part, acts[3], acts[4], peak)


STEP = 32


def fold_kernel(chunks, *refs):
    grad_ref, pair_ref = refs[-2:]
    peaks = refs[5 * len(chunks) : -2]

    squares = jnp.zeros((8, 128), F32)
    for k, (low, width) in enumerate(chunks):
        own, top_l, low_l, top_r, low_r = refs[5 * k : 5 * k + 5]

        def step(i, total, own=own, low=low, width=width, arms=((0, top_l, top_r), (HALF, low_l, low_r))):
            at = pl.multiple_of(i * STEP, STEP)
            for base, left, right in arms:
                rows = pl.ds(at, STEP)
                value = (
                    own[pl.ds(base + at, STEP), :]
                    + left[rows, :].astype(F32)
                    + right[rows, :].astype(F32)
                )
                grad_ref[pl.ds(base + at, STEP), low : low + width] = value
                square = (value * value).reshape(STEP // 8, 8, width).sum(axis=0)
                for j in range(width // 128):
                    total = total + square[:, j * 128 : (j + 1) * 128]
            return total

        squares = lax.fori_loop(0, HALF // STEP, step, squares)
    peak = peaks[0][...]
    for ref in peaks[1:]:
        peak = jnp.maximum(peak, ref[...])
    lane = lax.broadcasted_iota(jnp.int32, (128, 128), 1)
    pair_ref[...] = jnp.where(lane < 64, jnp.sum(squares), jnp.max(peak))


def fold_grad(parts, chunks, peaks):
    args = [v for part in parts for v in part] + list(peaks)
    return pl.pallas_call(
        functools.partial(fold_kernel, chunks),
        grid=(1,),
        in_specs=[pl.BlockSpec(v.shape, lambda i: (0, 0)) for v in args],
        out_specs=[
            pl.BlockSpec((S, C), lambda i: (0, 0)),
            pl.BlockSpec((128, 128), lambda i: (0, 0)),
        ],
        out_shape=[pltpu.HBM((S, C), F32), jax.ShapeDtypeStruct((128, 128), F32)],
        compiler_params=params(24),
        name="fold_grad",
    )(*args)


ROWS = 96


def adam_kernel(
    pairs_ref, grad_ref, moment_ref, second_ref, master_ref,
    moment_out, second_out, master_out, high_out, peak_out, again_ref, high_ref,
):
    i = pl.program_id(0)
    pairs = pairs_ref[...]
    squares = jnp.sum(pairs, axis=0, keepdims=True)[:, :1]
    clip_factor = jnp.minimum(1.0, jnp.sqrt(F32(OUT * IN)) / (jnp.sqrt(squares) + 1e-06))
    clipped = clip_factor * grad_ref[...]
    new_moment = 0.9 * moment_ref[...] + 0.1 * clipped
    new_second = 0.95 * second_ref[...] + 0.05 * clipped * clipped
    master = master_ref[...]
    new_master = master - 0.01 * (new_moment / (jnp.sqrt(new_second) + 1e-08) + 0.1 * master)
    moment_out[...] = new_moment
    second_out[...] = new_second
    master_out[...] = new_master
    again_ref[...] = new_master
    size = jnp.abs(new_master)
    high = size[:, :128]
    for j in range(1, C // 128):
        high = jnp.maximum(high, size[:, j * 128 : (j + 1) * 128])
    high_ref[pl.ds(pl.multiple_of(i * ROWS, ROWS), ROWS), :] = high

    @pl.when(i == S // ROWS - 1)
    def _():
        highs = jnp.max(high_ref[...].T, axis=0, keepdims=True)
        high_out[...] = jnp.broadcast_to(highs.reshape(1, 1, S), (8, 1, S))
        peak_out[...] = jnp.broadcast_to(jnp.max(pairs, axis=0, keepdims=True), (8, 128))


def adam(pairs, gradient, moment, second, master):
    block = pl.BlockSpec((ROWS, C), lambda i: (i, 0))
    small = jax.ShapeDtypeStruct((8, 128), F32)
    return pl.pallas_call(
        adam_kernel,
        grid=(S // ROWS,),
        in_specs=[pl.BlockSpec((128, 128), lambda i: (0, 0))] + [block] * 4,
        out_specs=[block] * 3
        + [whole((8, 1, S)), whole((8, 128)), block],
        out_shape=[jax.ShapeDtypeStruct((S, C), F32)] * 3
        + [jax.ShapeDtypeStruct((8, 1, S), F32), small, pltpu.VMEM((S, C), F32)],
        scratch_shapes=[pltpu.VMEM((S, 128), F32)],
        compiler_params=params(16),
        name="adam",
    )(pairs, gradient, moment, second, master)


def input_grad_kernel(count, own_last, *refs):
    rows, weights, outs = refs[:count], refs[count : count + 5], refs[count + 5 :]

    def step(i, carry):
        at = pl.ds(pl.multiple_of(i * NT, NT), NT)
        right = jnp.concatenate([w[:, at] for w in weights], axis=0)
        for k in range(count):
            total = jnp.dot(rows[k][0], right, preferred_element_type=F32)
            if own_last:
                outs[k][:, at] = total
            else:
                outs[2 * k][:, at] = total[:HALF].astype(BF)
                outs[2 * k + 1][:, at] = total[HALF:].astype(BF)
        return carry

    lax.fori_loop(0, C // NT, step, 0)


def input_grad(rows, blocks, weights, own):
    half = jax.ShapeDtypeStruct((HALF, C), BF)
    outs = [jax.ShapeDtypeStruct((S, C), F32)] if own else [half] * (2 * len(blocks))

    def piece(k):
        return pl.BlockSpec((1, S, C), lambda i: (k, 0, 0))

    def whole(v):
        return pl.BlockSpec(v.shape, lambda i: (0, 0))

    return pl.pallas_call(
        functools.partial(input_grad_kernel, len(blocks), own),
        grid=(1,),
        in_specs=[piece(k) for k in blocks] + [whole(v) for v in weights],
        out_specs=[whole(v) for v in outs],
        out_shape=outs,
        compiler_params=params(24),
        cost_estimate=pl.CostEstimate(
            flops=2 * len(blocks) * S * C * C, bytes_accessed=9 << 20, transcendentals=0
        ),
        name="input_grad",
    )(*([rows] * len(blocks)), *weights)


def codes_kernel(highs_ref, master_ref, codes_ref, scales_ref):
    row_peak = jnp.max(highs_ref[...], axis=0) + 1e-06
    scales_ref[...] = row_peak
    column = jnp.broadcast_to(row_peak, (128, S)).T
    for j in range(C // 128):
        at = slice(j * 128, (j + 1) * 128)
        codes_ref[:, at] = (master_ref[:, at] / column).astype(BF)


def codes(highs, master):
    return pl.pallas_call(
        codes_kernel,
        grid=(1,),
        in_specs=[whole((8, 1, S)), whole((S, C))],
        out_specs=[whole((S, C)), whole((1, S))],
        out_shape=[jax.ShapeDtypeStruct((S, C), BF), jax.ShapeDtypeStruct((1, S), F32)],
        compiler_params=params(16),
        name="codes",
    )(highs, master)


def ring_gather(v, axis):
    left = shift(v, axis, 1)
    right = shift(v, axis, -1)
    top = shift(left[:HALF], axis, 1)
    bottom = shift(right[HALF:], axis, -1)
    return v, left, right, top, bottom


def ring_scatter(far, near, axis):
    up_a, up_b, down_a, down_b = near
    from_left = shift(far[0], axis, 1)
    from_right = shift(far[1], axis, -1)
    left_b = shift(up_b, axis, 1)
    right_a = shift(down_a, axis, -1)
    up_a = (up_a.astype(F32) + from_left.astype(F32)).astype(BF)
    down_b = (down_b.astype(F32) + from_right.astype(F32)).astype(BF)
    left_a = shift(up_a, axis, 1)
    right_b = shift(down_b, axis, -1)
    return left_a, left_b, right_a, right_b


CHUNKS = ((0, C),)


def step(inputs, out_grad, weight_codes, weight_scales, master, moment, second):
    to_up, to_down, to_far = split_grads(
        pltpu.with_memory_space_constraint(out_grad, pltpu.HBM)
    )
    mine = [shift(to_up, "x", 1), shift(to_down, "x", -1), shift(to_far, "x", 2)]
    mine = jnp.concatenate(mine, axis=0)
    acts = [ring_gather(inputs[:, low : low + width], "x") for low, width in CHUNKS]
    held = [mine] + [shift(mine, "y", s) for s in (1, -1, 2)]
    other = [shift(v, "c", 1) for v in held]
    rows, cols = assemble(out_grad, held + other)

    weight = (weight_codes.astype(F32) * weight_scales.astype(F32)[:, None]).astype(BF)
    ring = ring_gather(weight, "z")
    weights = (*ring[3:], ring[2], ring[1], ring[0])

    parts, peaks = [], []
    for act in acts:
        far_a, far_b, peak_a = weight_grad_far(cols, act)
        *near, own, peak_b = weight_grad(cols, (1, 2, 3), act)
        peaks += [peak_a, peak_b]
        parts.append((own, *ring_scatter((far_a, far_b), near, "z")))

    rows, _ = lax.optimization_barrier((rows, own))
    i_far = input_grad(rows, (3,), weights, False)
    i_near = input_grad(rows, (2, 1), weights, False)
    (i_own,) = input_grad(rows, (0,), weights, True)
    left_a, left_b, right_a, right_b = ring_scatter(i_far, i_near, "x")
    top = i_own[:HALF] + left_a.astype(F32) + right_a.astype(F32)
    bottom = i_own[HALF:] + left_b.astype(F32) + right_b.astype(F32)
    grad_input = jnp.concatenate([top, bottom], axis=0).astype(BF)

    gradient, pair = fold_grad(parts, CHUNKS, peaks)
    pairs = lax.all_to_all(pair, ALL, 0, 0, tiled=True)
    gradient, moment, second, master = (
        pltpu.with_memory_space_constraint(v, pltpu.HBM)
        for v in (gradient, moment, second, master)
    )
    pairs, grad_input = lax.optimization_barrier((pairs, grad_input))
    new_moment, new_second, new_master, high, peak, again = adam(
        pairs, gradient, moment, second, master
    )
    highs = lax.all_to_all(high, TENSOR, 0, 0, tiled=True)
    new_codes, row_peak = codes(highs, pltpu.with_memory_space_constraint(again, pltpu.VMEM))
    new_scales = row_peak[0].astype(BF)
    return (grad_input, new_master, new_moment, new_second, new_codes, new_scales, peak[0, 64])


def solution(mesh):
    finer = Mesh(mesh.devices.reshape(4, 4, 4, 2), ALL)
    tiled = P(DP, TENSOR)
    in_specs = (tiled, P(DP, None), tiled, P(DP), tiled, tiled, tiled)
    out_specs = (tiled, tiled, tiled, tiled, tiled, P(DP), P())
    return jax.shard_map(step, mesh=finer, in_specs=in_specs, out_specs=out_specs, check_vma=False)
```

```python
import functools
import jax
import jax.numpy as jnp
from jax import lax
from jax.experimental import pallas as pl
from jax.experimental.pallas import tpu as pltpu
from jax.sharding import Mesh
from jax.sharding import PartitionSpec as P

ALL = ("z", "x", "y", "c")
DP = ("z", "x")
TENSOR = ("y", "c")
IN = 12288
OUT = 6144
S = 384
C = 1536
HALF = S // 2
SUB = S // 8
NT = 256
BF = jnp.bfloat16
F32 = jnp.float32
RZ = (2, 1, 3, 0)


def shift(v, axis, by):
    n = 4 if axis != "c" else 2
    return lax.ppermute(v, axis, [(i, (i + by) % n) for i in range(n)])


def params(mib):
    return pltpu.CompilerParams(vmem_limit_bytes=mib << 20)


def split_kernel(grad_ref, *refs):
    outs, slab, sem = refs[:3], refs[3], refs[4]
    z, x, y, c = (lax.axis_index(a) for a in ALL)
    top = pl.multiple_of((y * 2 + c) * SUB, SUB)
    copy = pltpu.make_async_copy(grad_ref.at[pl.ds(top, SUB), :], slab, sem)
    copy.start()
    copy.wait()
    for out, rx in zip(outs, (1, 3, 2)):
        for k, rz in enumerate(RZ):
            block = lax.rem(z + rz, 4) * 4 + lax.rem(x + rx, 4)
            out[:, k * S : (k + 1) * S] = slab[:, pl.ds(pl.multiple_of(block * S, S), S)]


def split_grads(out_grad):
    piece = jax.ShapeDtypeStruct((SUB, C), BF)
    return pl.pallas_call(
        split_kernel,
        in_specs=[pl.BlockSpec(memory_space=pltpu.HBM)],
        out_specs=[pl.BlockSpec(memory_space=pltpu.VMEM)] * 3,
        out_shape=[piece] * 3,
        scratch_shapes=[pltpu.VMEM((SUB, OUT), BF), pltpu.SemaphoreType.DMA],
        compiler_params=params(8),
        name="split_grads",
    )(out_grad)


def assemble_kernel(*refs):
    grad_ref, chunks, (rows_ref, cols_ref) = refs[0], refs[1:9], refs[9:]
    z, x, y, c = (lax.axis_index(a) for a in ALL)
    for k, rz in enumerate(RZ):
        block = lax.rem(z + rz, 4) * 4 + x
        rows_ref[0, :, k * S : (k + 1) * S] = grad_ref[:, pl.ds(pl.multiple_of(block * S, S), S)]
    for core in range(2):
        for i, ry in enumerate((0, 3, 1, 2)):
            source = lax.rem(y + ry, 4) * 2 + lax.rem(c + core, 2)
            top = pl.multiple_of(source * SUB, SUB)
            for j in range(3):
                rows_ref[1 + j, pl.ds(top, SUB), :] = chunks[core * 4 + i][
                    j * SUB : (j + 1) * SUB, :
                ]
    for j in range(4):
        for k in range(4):
            cols_ref[k, :, j * S : (j + 1) * S] = rows_ref[j, :, k * S : (k + 1) * S].T


def assemble(out_grad, chunks):
    full = pl.BlockSpec((3 * SUB, C), lambda i: (0, 0))
    out = pl.BlockSpec((4, S, C), lambda i: (0, 0, 0))
    return pl.pallas_call(
        assemble_kernel,
        grid=(1,),
        in_specs=[pl.BlockSpec((S, OUT), lambda i: (0, 0))] + [full] * 8,
        out_specs=[out, out],
        out_shape=[jax.ShapeDtypeStruct((4, S, C), BF)] * 2,
        compiler_params=params(28),
        name="assemble_grads",
    )(out_grad, *chunks)


def weight_grad_kernel(blocks, width, *refs):
    count = len(blocks)
    cols, acts, outs = refs[:count], refs[count : count + 5], refs[count + 5 :]
    peak_ref = outs[-1]
    peak_ref[...] = jnp.zeros_like(peak_ref)

    def step(i, carry):
        at = pl.ds(pl.multiple_of(i * NT, NT), NT)
        right = [acts[j][:, at] for j in range(3)]
        right.append(jnp.concatenate([acts[3][:, at], acts[4][:, at]], axis=0))
        peak = peak_ref[...]
        n = 0
        for k, block in enumerate(blocks):
            total = None
            for j in range(4):
                part = jnp.dot(
                    cols[k][0, :, j * S : (j + 1) * S], right[j], preferred_element_type=F32
                )
                high = jnp.max(jnp.abs(part).reshape(S // 8, 8, NT), axis=0)
                peak = jnp.maximum(peak, high)
                total = part if total is None else total + part
            if block == 3:
                outs[n][:, at] = total
                n += 1
            else:
                outs[n][:, at] = total[:HALF].astype(BF)
                outs[n + 1][:, at] = total[HALF:].astype(BF)
                n += 2
        peak_ref[...] = peak
        return carry

    lax.fori_loop(0, width // NT, step, 0)


def weight_grad(cols, blocks, acts):
    width = acts[0].shape[1]
    outs = []
    for block in blocks:
        if block == 3:
            outs.append(jax.ShapeDtypeStruct((S, width), F32))
        else:
            outs += [jax.ShapeDtypeStruct((HALF, width), BF)] * 2
    outs.append(jax.ShapeDtypeStruct((8, NT), F32))

    def piece(k):
        return pl.BlockSpec((1, S, C), lambda i: (k, 0, 0))

    def whole(v):
        return pl.BlockSpec(v.shape, lambda i: (0, 0))

    return pl.pallas_call(
        functools.partial(weight_grad_kernel, blocks, width),
        grid=(1,),
        in_specs=[piece(k) for k in blocks] + [whole(v) for v in acts],
        out_specs=[whole(v) for v in outs],
        out_shape=outs,
        compiler_params=params(24),
        cost_estimate=pl.CostEstimate(
            flops=2 * len(blocks) * S * C * width, bytes_accessed=9 << 20, transcendentals=0
        ),
        name="weight_grad",
    )(*([cols] * len(blocks)), *acts)


def far_start_kernel(cols_ref, own_ref, left_ref, right_ref, part_ref, peak_ref):
    peak_ref[...] = jnp.zeros_like(peak_ref)

    def step(i, carry):
        at = pl.ds(pl.multiple_of(i * NT, NT), NT)
        peak, total = peak_ref[...], None
        for j, ref in enumerate((own_ref, left_ref, right_ref)):
            part = jnp.dot(
                cols_ref[0, :, j * S : (j + 1) * S], ref[:, at], preferred_element_type=F32
            )
            peak = jnp.maximum(peak, jnp.max(jnp.abs(part).reshape(S // 8, 8, NT), axis=0))
            total = part if total is None else total + part
        part_ref[:, at] = total
        peak_ref[...] = peak
        return carry

    lax.fori_loop(0, C // NT, step, 0)


def far_finish_kernel(cols_ref, part_ref, top_ref, low_ref, peak_in, high_ref, low_out, peak_ref):
    peak_ref[...] = peak_in[...]

    def step(i, carry):
        at = pl.ds(pl.multiple_of(i * NT, NT), NT)
        right = jnp.concatenate([top_ref[:, at], low_ref[:, at]], axis=0)
        part = jnp.dot(cols_ref[0], right, preferred_element_type=F32)
        high = jnp.max(jnp.abs(part).reshape(S // 8, 8, NT), axis=0)
        peak_ref[...] = jnp.maximum(peak_ref[...], high)
        total = part_ref[:, at] + part
        high_ref[:, at] = total[:HALF].astype(BF)
        low_out[:, at] = total[HALF:].astype(BF)
        return carry

    lax.fori_loop(0, C // NT, step, 0)


def whole(shape):
    return pl.BlockSpec(shape, lambda i: (0,) * len(shape))


def weight_grad_far(cols, acts):
    small = jax.ShapeDtypeStruct((8, NT), F32)
    half = jax.ShapeDtypeStruct((HALF, C), BF)
    part, peak = pl.pallas_call(
        far_start_kernel,
        grid=(1,),
        in_specs=[whole((1, S, C))] + [whole((S, C))] * 3,
        out_specs=[whole((S, C)), whole((8, NT))],
        out_shape=[jax.ShapeDtypeStruct((S, C), F32), small],
        compiler_params=params(24),
        cost_estimate=pl.CostEstimate(
            flops=6 * S * S * C, bytes_accessed=6 << 20, transcendentals=0
        ),
        name="far_start",
    )(cols, *acts[:3])
    return pl.pallas_call(
        far_finish_kernel,
        grid=(1,),
        in_specs=[
            pl.BlockSpec((1, S, S), lambda i: (0, 0, 3)),
            whole((S, C)),
            whole((HALF, C)),
            whole((HALF, C)),
            whole((8, NT)),
        ],
        out_specs=[whole((HALF, C)), whole((HALF, C)), whole((8, NT))],
        out_shape=[half, half, small],
        compiler_params=params(24),
        cost_estimate=pl.CostEstimate(
            flops=2 * S * S * C, bytes_accessed=4 << 20, transcendentals=0
        ),
        name="far_finish",
    )(cols, part, acts[3], acts[4], peak)


STEP = 32


def fold_kernel(chunks, *refs):
    grad_ref, pair_ref = refs[-2:]
    peaks = refs[5 * len(chunks) : -2]

    squares = jnp.zeros((8, 128), F32)
    for k, (low, width) in enumerate(chunks):
        own, top_l, low_l, top_r, low_r = refs[5 * k : 5 * k + 5]

        def step(i, total, own=own, low=low, width=width, arms=((0, top_l, top_r), (HALF, low_l, low_r))):
            at = pl.multiple_of(i * STEP, STEP)
            for base, left, right in arms:
                rows = pl.ds(at, STEP)
                value = (
                    own[pl.ds(base + at, STEP), :]
                    + left[rows, :].astype(F32)
                    + right[rows, :].astype(F32)
                )
                grad_ref[pl.ds(base + at, STEP), low : low + width] = value
                square = (value * value).reshape(STEP // 8, 8, width).sum(axis=0)
                for j in range(width // 128):
                    total = total + square[:, j * 128 : (j + 1) * 128]
            return total

        squares = lax.fori_loop(0, HALF // STEP, step, squares)
    peak = peaks[0][...]
    for ref in peaks[1:]:
        peak = jnp.maximum(peak, ref[...])
    lane = lax.broadcasted_iota(jnp.int32, (128, 128), 1)
    pair_ref[...] = jnp.where(lane < 64, jnp.sum(squares), jnp.max(peak))


def fold_grad(parts, chunks, peaks):
    args = [v for part in parts for v in part] + list(peaks)
    return pl.pallas_call(
        functools.partial(fold_kernel, chunks),
        grid=(1,),
        in_specs=[pl.BlockSpec(v.shape, lambda i: (0, 0)) for v in args],
        out_specs=[
            pl.BlockSpec((S, C), lambda i: (0, 0)),
            pl.BlockSpec((128, 128), lambda i: (0, 0)),
        ],
        out_shape=[pltpu.HBM((S, C), F32), pltpu.HBM((128, 128), F32)],
        compiler_params=params(24),
        name="fold_grad",
    )(*args)


ROWS = 96


def adam_kernel(
    pairs_ref, grad_ref, moment_ref, second_ref, master_ref,
    moment_out, second_out, master_out, high_out, peak_out, again_ref, high_ref,
):
    i = pl.program_id(0)
    pairs = pairs_ref[...]
    squares = jnp.sum(pairs, axis=0, keepdims=True)[:, :1]
    clip_factor = jnp.minimum(1.0, jnp.sqrt(F32(OUT * IN)) / (jnp.sqrt(squares) + 1e-06))
    clipped = clip_factor * grad_ref[...]
    new_moment = 0.9 * moment_ref[...] + 0.1 * clipped
    new_second = 0.95 * second_ref[...] + 0.05 * clipped * clipped
    master = master_ref[...]
    new_master = master - 0.01 * (new_moment / (jnp.sqrt(new_second) + 1e-08) + 0.1 * master)
    moment_out[...] = new_moment
    second_out[...] = new_second
    master_out[...] = new_master
    again_ref[...] = new_master
    size = jnp.abs(new_master)
    high = size[:, :128]
    for j in range(1, C // 128):
        high = jnp.maximum(high, size[:, j * 128 : (j + 1) * 128])
    high_ref[pl.ds(pl.multiple_of(i * ROWS, ROWS), ROWS), :] = high

    @pl.when(i == S // ROWS - 1)
    def _():
        highs = jnp.max(high_ref[...].T, axis=0, keepdims=True)
        high_out[...] = jnp.broadcast_to(highs.reshape(1, 1, S), (8, 1, S))
        peak_out[...] = jnp.broadcast_to(jnp.max(pairs, axis=0, keepdims=True), (8, 128))


def adam(pairs, gradient, moment, second, master):
    block = pl.BlockSpec((ROWS, C), lambda i: (i, 0))
    small = jax.ShapeDtypeStruct((8, 128), F32)
    return pl.pallas_call(
        adam_kernel,
        grid=(S // ROWS,),
        in_specs=[pl.BlockSpec((128, 128), lambda i: (0, 0))] + [block] * 4,
        out_specs=[block] * 3
        + [whole((8, 1, S)), whole((8, 128)), block],
        out_shape=[jax.ShapeDtypeStruct((S, C), F32)] * 3
        + [jax.ShapeDtypeStruct((8, 1, S), F32), small, pltpu.VMEM((S, C), F32)],
        scratch_shapes=[pltpu.VMEM((S, 128), F32)],
        compiler_params=params(16),
        name="adam",
    )(pairs, gradient, moment, second, master)


def input_grad_kernel(count, own_last, *refs):
    rows, weights, outs = refs[:count], refs[count : count + 5], refs[count + 5 :]

    def step(i, carry):
        at = pl.ds(pl.multiple_of(i * NT, NT), NT)
        right = jnp.concatenate([w[:, at] for w in weights], axis=0)
        for k in range(count):
            total = jnp.dot(rows[k][0], right, preferred_element_type=F32)
            if own_last:
                outs[k][:, at] = total
            else:
                outs[2 * k][:, at] = total[:HALF].astype(BF)
                outs[2 * k + 1][:, at] = total[HALF:].astype(BF)
        return carry

    lax.fori_loop(0, C // NT, step, 0)


def input_grad(rows, blocks, weights, own):
    half = jax.ShapeDtypeStruct((HALF, C), BF)
    outs = [pltpu.HBM((S, C), F32)] if own else [half] * (2 * len(blocks))

    def piece(k):
        return pl.BlockSpec((1, S, C), lambda i: (k, 0, 0))

    def whole(v):
        return pl.BlockSpec(v.shape, lambda i: (0, 0))

    return pl.pallas_call(
        functools.partial(input_grad_kernel, len(blocks), own),
        grid=(1,),
        in_specs=[piece(k) for k in blocks] + [whole(v) for v in weights],
        out_specs=[whole(v) for v in outs],
        out_shape=outs,
        compiler_params=params(24),
        cost_estimate=pl.CostEstimate(
            flops=2 * len(blocks) * S * C * C, bytes_accessed=9 << 20, transcendentals=0
        ),
        name="input_grad",
    )(*([rows] * len(blocks)), *weights)


def codes_kernel(highs_ref, master_ref, codes_ref, scales_ref):
    row_peak = jnp.max(highs_ref[...], axis=0) + 1e-06
    scales_ref[...] = row_peak
    column = jnp.broadcast_to(row_peak, (128, S)).T
    for j in range(C // 128):
        at = slice(j * 128, (j + 1) * 128)
        codes_ref[:, at] = (master_ref[:, at] / column).astype(BF)


def codes(highs, master):
    return pl.pallas_call(
        codes_kernel,
        grid=(1,),
        in_specs=[whole((8, 1, S)), whole((S, C))],
        out_specs=[whole((S, C)), whole((1, S))],
        out_shape=[jax.ShapeDtypeStruct((S, C), BF), jax.ShapeDtypeStruct((1, S), F32)],
        compiler_params=params(16),
        name="codes",
    )(highs, master)


def ring_gather(v, axis):
    left = shift(v, axis, 1)
    right = shift(v, axis, -1)
    top = shift(left[:HALF], axis, 1)
    bottom = shift(right[HALF:], axis, -1)
    return v, left, right, top, bottom


def ring_scatter(far, near, axis):
    up_a, up_b, down_a, down_b = near
    from_left = shift(far[0], axis, 1)
    from_right = shift(far[1], axis, -1)
    left_b = shift(up_b, axis, 1)
    right_a = shift(down_a, axis, -1)
    up_a = (up_a.astype(F32) + from_left.astype(F32)).astype(BF)
    down_b = (down_b.astype(F32) + from_right.astype(F32)).astype(BF)
    left_a = shift(up_a, axis, 1)
    right_b = shift(down_b, axis, -1)
    return left_a, left_b, right_a, right_b


CHUNKS = ((0, C),)


def step(inputs, out_grad, weight_codes, weight_scales, master, moment, second):
    to_up, to_down, to_far = split_grads(
        pltpu.with_memory_space_constraint(out_grad, pltpu.HBM)
    )
    mine = [shift(to_up, "x", 1), shift(to_down, "x", -1), shift(to_far, "x", 2)]
    mine = jnp.concatenate(mine, axis=0)
    acts = [ring_gather(inputs[:, low : low + width], "x") for low, width in CHUNKS]
    held = [mine] + [shift(mine, "y", s) for s in (1, -1, 2)]
    other = [shift(v, "c", 1) for v in held]
    rows, cols = assemble(out_grad, held + other)

    weight = (weight_codes.astype(F32) * weight_scales.astype(F32)[:, None]).astype(BF)
    ring = ring_gather(weight, "z")
    weights = (*ring[3:], ring[2], ring[1], ring[0])

    parts, peaks = [], []
    for act in acts:
        far_a, far_b, peak_a = weight_grad_far(cols, act)
        *near, own, peak_b = weight_grad(cols, (1, 2, 3), act)
        peaks += [peak_a, peak_b]
        parts.append((own, *ring_scatter((far_a, far_b), near, "z")))

    rows, _ = lax.optimization_barrier((rows, own))
    i_far = input_grad(rows, (3,), weights, False)
    i_near = input_grad(rows, (2, 1), weights, False)
    (i_own,) = input_grad(rows, (0,), weights, True)
    left_a, left_b, right_a, right_b = ring_scatter(i_far, i_near, "x")
    top = i_own[:HALF] + left_a.astype(F32) + right_a.astype(F32)
    bottom = i_own[HALF:] + left_b.astype(F32) + right_b.astype(F32)
    grad_input = jnp.concatenate([top, bottom], axis=0).astype(BF)
    gradient, pair = fold_grad(parts, CHUNKS, peaks)
    pairs = lax.all_to_all(pair, ALL, 0, 0, tiled=True)
    gradient, moment, second, master = (
        pltpu.with_memory_space_constraint(v, pltpu.HBM)
        for v in (gradient, moment, second, master)
    )
    new_moment, new_second, new_master, high, peak, again = adam(
        pairs, gradient, moment, second, master
    )
    highs = lax.all_to_all(high, TENSOR, 0, 0, tiled=True)
    highs, grad_input = lax.optimization_barrier((highs, grad_input))
    new_codes, row_peak = codes(highs, pltpu.with_memory_space_constraint(again, pltpu.VMEM))
    new_scales = row_peak[0].astype(BF)
    return (grad_input, new_master, new_moment, new_second, new_codes, new_scales, peak[0, 64])


def solution(mesh):
    finer = Mesh(mesh.devices.reshape(4, 4, 4, 2), ALL)
    tiled = P(DP, TENSOR)
    in_specs = (tiled, P(DP, None), tiled, P(DP), tiled, tiled, tiled)
    out_specs = (tiled, tiled, tiled, tiled, tiled, P(DP), P())
    return jax.shard_map(step, mesh=finer, in_specs=in_specs, out_specs=out_specs, check_vma=False)
```

```python
import functools
import jax
import jax.numpy as jnp
from jax import lax
from jax.experimental import pallas as pl
from jax.experimental.pallas import tpu as pltpu
from jax.sharding import Mesh
from jax.sharding import PartitionSpec as P

ALL = ("z", "x", "y", "c")
DP = ("z", "x")
TENSOR = ("y", "c")
IN = 12288
OUT = 6144
S = 384
C = 1536
HALF = S // 2
SUB = S // 8
NT = 256
BF = jnp.bfloat16
F32 = jnp.float32
RZ = (2, 1, 3, 0)


def shift(v, axis, by):
    n = 4 if axis != "c" else 2
    return lax.ppermute(v, axis, [(i, (i + by) % n) for i in range(n)])


def params(mib):
    return pltpu.CompilerParams(vmem_limit_bytes=mib << 20)


def split_kernel(grad_ref, *refs):
    outs, slab, sem = refs[:3], refs[3], refs[4]
    z, x, y, c = (lax.axis_index(a) for a in ALL)
    top = pl.multiple_of((y * 2 + c) * SUB, SUB)
    copy = pltpu.make_async_copy(grad_ref.at[pl.ds(top, SUB), :], slab, sem)
    copy.start()
    copy.wait()
    for out, rx in zip(outs, (1, 3, 2)):
        for k, rz in enumerate(RZ):
            block = lax.rem(z + rz, 4) * 4 + lax.rem(x + rx, 4)
            out[:, k * S : (k + 1) * S] = slab[:, pl.ds(pl.multiple_of(block * S, S), S)]


def split_grads(out_grad):
    piece = jax.ShapeDtypeStruct((SUB, C), BF)
    return pl.pallas_call(
        split_kernel,
        in_specs=[pl.BlockSpec(memory_space=pltpu.HBM)],
        out_specs=[pl.BlockSpec(memory_space=pltpu.VMEM)] * 3,
        out_shape=[piece] * 3,
        scratch_shapes=[pltpu.VMEM((SUB, OUT), BF), pltpu.SemaphoreType.DMA],
        compiler_params=params(8),
        name="split_grads",
    )(out_grad)


def assemble_kernel(*refs):
    grad_ref, chunks, (rows_ref, cols_ref) = refs[0], refs[1:9], refs[9:]
    z, x, y, c = (lax.axis_index(a) for a in ALL)
    for k, rz in enumerate(RZ):
        block = lax.rem(z + rz, 4) * 4 + x
        rows_ref[0, :, k * S : (k + 1) * S] = grad_ref[:, pl.ds(pl.multiple_of(block * S, S), S)]
    for core in range(2):
        for i, ry in enumerate((0, 3, 1, 2)):
            source = lax.rem(y + ry, 4) * 2 + lax.rem(c + core, 2)
            top = pl.multiple_of(source * SUB, SUB)
            for j in range(3):
                rows_ref[1 + j, pl.ds(top, SUB), :] = chunks[core * 4 + i][
                    j * SUB : (j + 1) * SUB, :
                ]
    for j in range(4):
        for k in range(4):
            cols_ref[k, :, j * S : (j + 1) * S] = rows_ref[j, :, k * S : (k + 1) * S].T


def assemble(out_grad, chunks):
    full = pl.BlockSpec((3 * SUB, C), lambda i: (0, 0))
    out = pl.BlockSpec((4, S, C), lambda i: (0, 0, 0))
    return pl.pallas_call(
        assemble_kernel,
        grid=(1,),
        in_specs=[pl.BlockSpec((S, OUT), lambda i: (0, 0))] + [full] * 8,
        out_specs=[out, out],
        out_shape=[jax.ShapeDtypeStruct((4, S, C), BF)] * 2,
        compiler_params=params(28),
        name="assemble_grads",
    )(out_grad, *chunks)


def weight_grad_kernel(blocks, width, *refs):
    count = len(blocks)
    cols, acts, outs = refs[:count], refs[count : count + 5], refs[count + 5 :]
    peak_ref = outs[-1]
    peak_ref[...] = jnp.zeros_like(peak_ref)

    def step(i, carry):
        at = pl.ds(pl.multiple_of(i * NT, NT), NT)
        right = [acts[j][:, at] for j in range(3)]
        right.append(jnp.concatenate([acts[3][:, at], acts[4][:, at]], axis=0))
        peak = peak_ref[...]
        n = 0
        for k, block in enumerate(blocks):
            total = None
            for j in range(4):
                part = jnp.dot(
                    cols[k][0, :, j * S : (j + 1) * S], right[j], preferred_element_type=F32
                )
                high = jnp.max(jnp.abs(part).reshape(S // 8, 8, NT), axis=0)
                peak = jnp.maximum(peak, high)
                total = part if total is None else total + part
            if block == 3:
                outs[n][:, at] = total
                n += 1
            else:
                outs[n][:, at] = total[:HALF].astype(BF)
                outs[n + 1][:, at] = total[HALF:].astype(BF)
                n += 2
        peak_ref[...] = peak
        return carry

    lax.fori_loop(0, width // NT, step, 0)


def weight_grad(cols, blocks, acts):
    width = acts[0].shape[1]
    outs = []
    for block in blocks:
        if block == 3:
            outs.append(jax.ShapeDtypeStruct((S, width), F32))
        else:
            outs += [jax.ShapeDtypeStruct((HALF, width), BF)] * 2
    outs.append(jax.ShapeDtypeStruct((8, NT), F32))

    def piece(k):
        return pl.BlockSpec((1, S, C), lambda i: (k, 0, 0))

    def whole(v):
        return pl.BlockSpec(v.shape, lambda i: (0, 0))

    return pl.pallas_call(
        functools.partial(weight_grad_kernel, blocks, width),
        grid=(1,),
        in_specs=[piece(k) for k in blocks] + [whole(v) for v in acts],
        out_specs=[whole(v) for v in outs],
        out_shape=outs,
        compiler_params=params(24),
        cost_estimate=pl.CostEstimate(
            flops=2 * len(blocks) * S * C * width, bytes_accessed=9 << 20, transcendentals=0
        ),
        name="weight_grad",
    )(*([cols] * len(blocks)), *acts)


def far_start_kernel(cols_ref, own_ref, left_ref, right_ref, part_ref, peak_ref):
    peak_ref[...] = jnp.zeros_like(peak_ref)

    def step(i, carry):
        at = pl.ds(pl.multiple_of(i * NT, NT), NT)
        peak, total = peak_ref[...], None
        for j, ref in enumerate((own_ref, left_ref, right_ref)):
            part = jnp.dot(
                cols_ref[0, :, j * S : (j + 1) * S], ref[:, at], preferred_element_type=F32
            )
            peak = jnp.maximum(peak, jnp.max(jnp.abs(part).reshape(S // 8, 8, NT), axis=0))
            total = part if total is None else total + part
        part_ref[:, at] = total
        peak_ref[...] = peak
        return carry

    lax.fori_loop(0, C // NT, step, 0)


def far_finish_kernel(cols_ref, part_ref, top_ref, low_ref, peak_in, high_ref, low_out, peak_ref):
    peak_ref[...] = peak_in[...]

    def step(i, carry):
        at = pl.ds(pl.multiple_of(i * NT, NT), NT)
        right = jnp.concatenate([top_ref[:, at], low_ref[:, at]], axis=0)
        part = jnp.dot(cols_ref[0], right, preferred_element_type=F32)
        high = jnp.max(jnp.abs(part).reshape(S // 8, 8, NT), axis=0)
        peak_ref[...] = jnp.maximum(peak_ref[...], high)
        total = part_ref[:, at] + part
        high_ref[:, at] = total[:HALF].astype(BF)
        low_out[:, at] = total[HALF:].astype(BF)
        return carry

    lax.fori_loop(0, C // NT, step, 0)


def whole(shape):
    return pl.BlockSpec(shape, lambda i: (0,) * len(shape))


def weight_grad_far(cols, acts):
    small = jax.ShapeDtypeStruct((8, NT), F32)
    half = jax.ShapeDtypeStruct((HALF, C), BF)
    part, peak = pl.pallas_call(
        far_start_kernel,
        grid=(1,),
        in_specs=[whole((1, S, C))] + [whole((S, C))] * 3,
        out_specs=[whole((S, C)), whole((8, NT))],
        out_shape=[jax.ShapeDtypeStruct((S, C), F32), small],
        compiler_params=params(24),
        cost_estimate=pl.CostEstimate(
            flops=6 * S * S * C, bytes_accessed=6 << 20, transcendentals=0
        ),
        name="far_start",
    )(cols, *acts[:3])
    return pl.pallas_call(
        far_finish_kernel,
        grid=(1,),
        in_specs=[
            pl.BlockSpec((1, S, S), lambda i: (0, 0, 3)),
            whole((S, C)),
            whole((HALF, C)),
            whole((HALF, C)),
            whole((8, NT)),
        ],
        out_specs=[whole((HALF, C)), whole((HALF, C)), whole((8, NT))],
        out_shape=[half, half, small],
        compiler_params=params(24),
        cost_estimate=pl.CostEstimate(
            flops=2 * S * S * C, bytes_accessed=4 << 20, transcendentals=0
        ),
        name="far_finish",
    )(cols, part, acts[3], acts[4], peak)


STEP = 32


def fold_kernel(chunks, *refs):
    grad_ref, pair_ref = refs[-2:]
    peaks = refs[5 * len(chunks) : -2]

    squares = jnp.zeros((8, 128), F32)
    for k, (low, width) in enumerate(chunks):
        own, top_l, low_l, top_r, low_r = refs[5 * k : 5 * k + 5]

        def step(i, total, own=own, low=low, width=width, arms=((0, top_l, top_r), (HALF, low_l, low_r))):
            at = pl.multiple_of(i * STEP, STEP)
            for base, left, right in arms:
                rows = pl.ds(at, STEP)
                value = (
                    own[pl.ds(base + at, STEP), :]
                    + left[rows, :].astype(F32)
                    + right[rows, :].astype(F32)
                )
                grad_ref[pl.ds(base + at, STEP), low : low + width] = value
                square = (value * value).reshape(STEP // 8, 8, width).sum(axis=0)
                for j in range(width // 128):
                    total = total + square[:, j * 128 : (j + 1) * 128]
            return total

        squares = lax.fori_loop(0, HALF // STEP, step, squares)
    peak = peaks[0][...]
    for ref in peaks[1:]:
        peak = jnp.maximum(peak, ref[...])
    lane = lax.broadcasted_iota(jnp.int32, (128, 128), 1)
    pair_ref[...] = jnp.where(lane < 64, jnp.sum(squares), jnp.max(peak))


def fold_grad(parts, chunks, peaks):
    args = [v for part in parts for v in part] + list(peaks)
    return pl.pallas_call(
        functools.partial(fold_kernel, chunks),
        grid=(1,),
        in_specs=[pl.BlockSpec(v.shape, lambda i: (0, 0)) for v in args],
        out_specs=[
            pl.BlockSpec((S, C), lambda i: (0, 0)),
            pl.BlockSpec((128, 128), lambda i: (0, 0)),
        ],
        out_shape=[pltpu.HBM((S, C), F32), jax.ShapeDtypeStruct((128, 128), F32)],
        compiler_params=params(24),
        name="fold_grad",
    )(*args)


ROWS = 96


def adam_kernel(
    pairs_ref, grad_ref, moment_ref, second_ref, master_ref,
    moment_out, second_out, master_out, high_out, peak_out, again_ref, high_ref,
):
    i = pl.program_id(0)
    pairs = pairs_ref[...]
    squares = jnp.sum(pairs, axis=0, keepdims=True)[:, :1]
    clip_factor = jnp.minimum(1.0, jnp.sqrt(F32(OUT * IN)) / (jnp.sqrt(squares) + 1e-06))
    clipped = clip_factor * grad_ref[...]
    new_moment = 0.9 * moment_ref[...] + 0.1 * clipped
    new_second = 0.95 * second_ref[...] + 0.05 * clipped * clipped
    master = master_ref[...]
    new_master = master - 0.01 * (new_moment / (jnp.sqrt(new_second) + 1e-08) + 0.1 * master)
    moment_out[...] = new_moment
    second_out[...] = new_second
    master_out[...] = new_master
    again_ref[...] = new_master
    size = jnp.abs(new_master)
    high = size[:, :128]
    for j in range(1, C // 128):
        high = jnp.maximum(high, size[:, j * 128 : (j + 1) * 128])
    high_ref[pl.ds(pl.multiple_of(i * ROWS, ROWS), ROWS), :] = high

    @pl.when(i == S // ROWS - 1)
    def _():
        highs = jnp.max(high_ref[...].T, axis=0, keepdims=True)
        high_out[...] = jnp.broadcast_to(highs.reshape(1, 1, S), (8, 1, S))
        peak_out[...] = jnp.broadcast_to(jnp.max(pairs, axis=0, keepdims=True), (8, 128))


def adam(pairs, gradient, moment, second, master):
    block = pl.BlockSpec((ROWS, C), lambda i: (i, 0))
    small = jax.ShapeDtypeStruct((8, 128), F32)
    return pl.pallas_call(
        adam_kernel,
        grid=(S // ROWS,),
        in_specs=[pl.BlockSpec((128, 128), lambda i: (0, 0))] + [block] * 4,
        out_specs=[block] * 3
        + [whole((8, 1, S)), whole((8, 128)), block],
        out_shape=[jax.ShapeDtypeStruct((S, C), F32)] * 3
        + [jax.ShapeDtypeStruct((8, 1, S), F32), small, pltpu.VMEM((S, C), F32)],
        scratch_shapes=[pltpu.VMEM((S, 128), F32)],
        compiler_params=params(16),
        name="adam",
    )(pairs, gradient, moment, second, master)


def input_grad_kernel(count, own_last, *refs):
    rows, weights, outs = refs[:count], refs[count : count + 5], refs[count + 5 :]

    def step(i, carry):
        at = pl.ds(pl.multiple_of(i * NT, NT), NT)
        right = jnp.concatenate([w[:, at] for w in weights], axis=0)
        for k in range(count):
            total = jnp.dot(rows[k][0], right, preferred_element_type=F32)
            if own_last or count == 2:
                outs[k][:, at] = total.astype(outs[k].dtype)
            else:
                outs[2 * k][:, at] = total[:HALF].astype(BF)
                outs[2 * k + 1][:, at] = total[HALF:].astype(BF)
        return carry

    lax.fori_loop(0, C // NT, step, 0)


def input_grad(rows, blocks, weights, own):
    half = jax.ShapeDtypeStruct((HALF, C), BF)
    outs = [pltpu.HBM((S, C), F32)] if own else [half] * (2 * len(blocks))
    if len(blocks) == 2:
        outs = [jax.ShapeDtypeStruct((S, C), BF)] * 2

    def piece(k):
        return pl.BlockSpec((1, S, C), lambda i: (k, 0, 0))

    def whole(v):
        return pl.BlockSpec(v.shape, lambda i: (0, 0))

    return pl.pallas_call(
        functools.partial(input_grad_kernel, len(blocks), own),
        grid=(1,),
        in_specs=[piece(k) for k in blocks] + [whole(v) for v in weights],
        out_specs=[whole(v) for v in outs],
        out_shape=outs,
        compiler_params=params(24),
        cost_estimate=pl.CostEstimate(
            flops=2 * len(blocks) * S * C * C, bytes_accessed=9 << 20, transcendentals=0
        ),
        name="input_grad",
    )(*([rows] * len(blocks)), *weights)


def codes_kernel(highs_ref, master_ref, codes_ref, scales_ref):
    row_peak = jnp.max(highs_ref[...], axis=0) + 1e-06
    scales_ref[...] = row_peak
    column = jnp.broadcast_to(row_peak, (128, S)).T
    for j in range(C // 128):
        at = slice(j * 128, (j + 1) * 128)
        codes_ref[:, at] = (master_ref[:, at] / column).astype(BF)


def codes(highs, master):
    return pl.pallas_call(
        codes_kernel,
        grid=(1,),
        in_specs=[whole((8, 1, S)), whole((S, C))],
        out_specs=[whole((S, C)), whole((1, S))],
        out_shape=[jax.ShapeDtypeStruct((S, C), BF), jax.ShapeDtypeStruct((1, S), F32)],
        compiler_params=params(16),
        name="codes",
    )(highs, master)


def ring_gather(v, axis):
    left = shift(v, axis, 1)
    right = shift(v, axis, -1)
    top = shift(left[:HALF], axis, 1)
    bottom = shift(right[HALF:], axis, -1)
    return v, left, right, top, bottom


def ring_scatter(far, near, axis):
    up_a, up_b, down_a, down_b = near
    from_left = shift(far[0], axis, 1)
    from_right = shift(far[1], axis, -1)
    left_b = shift(up_b, axis, 1)
    right_a = shift(down_a, axis, -1)
    up_a = (up_a.astype(F32) + from_left.astype(F32)).astype(BF)
    down_b = (down_b.astype(F32) + from_right.astype(F32)).astype(BF)
    left_a = shift(up_a, axis, 1)
    right_b = shift(down_b, axis, -1)
    return left_a, left_b, right_a, right_b


def ring_scatter_whole(far, near, axis):
    up, down = near
    from_left = shift(far[0], axis, 1)
    from_right = shift(far[1], axis, -1)
    up_a = (up[:HALF].astype(F32) + from_left.astype(F32)).astype(BF)
    down_b = (down[HALF:].astype(F32) + from_right.astype(F32)).astype(BF)
    up = lax.dynamic_update_slice(up, up_a, (0, 0))
    down = lax.dynamic_update_slice(down, down_b, (HALF, 0))
    return shift(up, axis, 1), shift(down, axis, -1)


CHUNKS = ((0, C),)


def step(inputs, out_grad, weight_codes, weight_scales, master, moment, second):
    to_up, to_down, to_far = split_grads(
        pltpu.with_memory_space_constraint(out_grad, pltpu.HBM)
    )
    mine = [shift(to_up, "x", 1), shift(to_down, "x", -1), shift(to_far, "x", 2)]
    mine = jnp.concatenate(mine, axis=0)
    acts = [ring_gather(inputs[:, low : low + width], "x") for low, width in CHUNKS]
    held = [mine] + [shift(mine, "y", s) for s in (1, -1, 2)]
    other = [shift(v, "c", 1) for v in held]
    rows, cols = assemble(out_grad, held + other)

    weight = (weight_codes.astype(F32) * weight_scales.astype(F32)[:, None]).astype(BF)
    ring = ring_gather(weight, "z")
    weights = (*ring[3:], ring[2], ring[1], ring[0])

    parts, peaks = [], []
    for act in acts:
        far_a, far_b, peak_a = weight_grad_far(cols, act)
        *near, own, peak_b = weight_grad(cols, (1, 2, 3), act)
        peaks += [peak_a, peak_b]
        parts.append((own, *ring_scatter((far_a, far_b), near, "z")))

    rows, _ = lax.optimization_barrier((rows, own))
    i_far = input_grad(rows, (3,), weights, False)
    i_near = input_grad(rows, (2, 1), weights, False)
    (i_own,) = input_grad(rows, (0,), weights, True)
    left, right = ring_scatter_whole(i_far, i_near, "x")
    peaks, i_own = lax.optimization_barrier((peaks, i_own))
    grad_input = (i_own + left.astype(F32) + right.astype(F32)).astype(BF)
    gradient, pair = fold_grad(parts, CHUNKS, peaks)
    pairs = lax.all_to_all(pair, ALL, 0, 0, tiled=True)
    gradient, moment, second, master = (
        pltpu.with_memory_space_constraint(v, pltpu.HBM)
        for v in (gradient, moment, second, master)
    )
    new_moment, new_second, new_master, high, peak, again = adam(
        pairs, gradient, moment, second, master
    )
    highs = lax.all_to_all(high, TENSOR, 0, 0, tiled=True)
    highs, grad_input = lax.optimization_barrier((highs, grad_input))
    new_codes, row_peak = codes(highs, pltpu.with_memory_space_constraint(again, pltpu.VMEM))
    new_scales = row_peak[0].astype(BF)
    return (grad_input, new_master, new_moment, new_second, new_codes, new_scales, peak[0, 64])


def solution(mesh):
    finer = Mesh(mesh.devices.reshape(4, 4, 4, 2), ALL)
    tiled = P(DP, TENSOR)
    in_specs = (tiled, P(DP, None), tiled, P(DP), tiled, tiled, tiled)
    out_specs = (tiled, tiled, tiled, tiled, tiled, P(DP), P())
    return jax.shard_map(step, mesh=finer, in_specs=in_specs, out_specs=out_specs, check_vma=False)
```

```python
import functools
import jax
import jax.numpy as jnp
from jax import lax
from jax.experimental import pallas as pl
from jax.experimental.pallas import tpu as pltpu
from jax.sharding import Mesh
from jax.sharding import PartitionSpec as P

ALL = ("z", "x", "y", "c")
DP = ("z", "x")
TENSOR = ("y", "c")
IN = 12288
OUT = 6144
S = 384
C = 1536
HALF = S // 2
SUB = S // 8
NT = 256
BF = jnp.bfloat16
F32 = jnp.float32
RZ = (2, 1, 3, 0)


def shift(v, axis, by):
    n = 4 if axis != "c" else 2
    return lax.ppermute(v, axis, [(i, (i + by) % n) for i in range(n)])


def params(mib):
    return pltpu.CompilerParams(vmem_limit_bytes=mib << 20)


def split_kernel(grad_ref, *refs):
    outs, slab, sem = refs[:3], refs[3], refs[4]
    z, x, y, c = (lax.axis_index(a) for a in ALL)
    top = pl.multiple_of((y * 2 + c) * SUB, SUB)
    copy = pltpu.make_async_copy(grad_ref.at[pl.ds(top, SUB), :], slab, sem)
    copy.start()
    copy.wait()
    for out, rx in zip(outs, (1, 3, 2)):
        for k, rz in enumerate(RZ):
            block = lax.rem(z + rz, 4) * 4 + lax.rem(x + rx, 4)
            out[:, k * S : (k + 1) * S] = slab[:, pl.ds(pl.multiple_of(block * S, S), S)]


def split_grads(out_grad):
    piece = jax.ShapeDtypeStruct((SUB, C), BF)
    return pl.pallas_call(
        split_kernel,
        in_specs=[pl.BlockSpec(memory_space=pltpu.HBM)],
        out_specs=[pl.BlockSpec(memory_space=pltpu.VMEM)] * 3,
        out_shape=[piece] * 3,
        scratch_shapes=[pltpu.VMEM((SUB, OUT), BF), pltpu.SemaphoreType.DMA],
        compiler_params=params(8),
        name="split_grads",
    )(out_grad)


def assemble_kernel(*refs):
    grad_ref, chunks, (rows_ref, cols_ref) = refs[0], refs[1:9], refs[9:]
    z, x, y, c = (lax.axis_index(a) for a in ALL)
    for k, rz in enumerate(RZ):
        block = lax.rem(z + rz, 4) * 4 + x
        rows_ref[0, :, k * S : (k + 1) * S] = grad_ref[:, pl.ds(pl.multiple_of(block * S, S), S)]
    for core in range(2):
        for i, ry in enumerate((0, 3, 1, 2)):
            source = lax.rem(y + ry, 4) * 2 + lax.rem(c + core, 2)
            top = pl.multiple_of(source * SUB, SUB)
            for j in range(3):
                rows_ref[1 + j, pl.ds(top, SUB), :] = chunks[core * 4 + i][
                    j * SUB : (j + 1) * SUB, :
                ]
    for j in range(4):
        for k in range(4):
            cols_ref[k, :, j * S : (j + 1) * S] = rows_ref[j, :, k * S : (k + 1) * S].T


def assemble(out_grad, chunks):
    full = pl.BlockSpec((3 * SUB, C), lambda i: (0, 0))
    out = pl.BlockSpec((4, S, C), lambda i: (0, 0, 0))
    return pl.pallas_call(
        assemble_kernel,
        grid=(1,),
        in_specs=[pl.BlockSpec((S, OUT), lambda i: (0, 0))] + [full] * 8,
        out_specs=[out, out],
        out_shape=[jax.ShapeDtypeStruct((4, S, C), BF)] * 2,
        compiler_params=params(28),
        name="assemble_grads",
    )(out_grad, *chunks)


def weight_grad_kernel(blocks, width, *refs):
    count = len(blocks)
    cols, acts, outs = refs[:count], refs[count : count + 5], refs[count + 5 :]
    peak_ref = outs[-1]
    peak_ref[...] = jnp.zeros_like(peak_ref)

    def step(i, carry):
        at = pl.ds(pl.multiple_of(i * NT, NT), NT)
        right = [acts[j][:, at] for j in range(3)]
        right.append(jnp.concatenate([acts[3][:, at], acts[4][:, at]], axis=0))
        peak = peak_ref[...]
        n = 0
        for k, block in enumerate(blocks):
            total = None
            for j in range(4):
                part = jnp.dot(
                    cols[k][0, :, j * S : (j + 1) * S], right[j], preferred_element_type=F32
                )
                high = jnp.max(jnp.abs(part).reshape(S // 8, 8, NT), axis=0)
                peak = jnp.maximum(peak, high)
                total = part if total is None else total + part
            if block == 3:
                outs[n][:, at] = total
                n += 1
            else:
                outs[n][:, at] = total[:HALF].astype(BF)
                outs[n + 1][:, at] = total[HALF:].astype(BF)
                n += 2
        peak_ref[...] = peak
        return carry

    lax.fori_loop(0, width // NT, step, 0)


def weight_grad(cols, blocks, acts):
    width = acts[0].shape[1]
    outs = []
    for block in blocks:
        if block == 3:
            outs.append(jax.ShapeDtypeStruct((S, width), F32))
        else:
            outs += [jax.ShapeDtypeStruct((HALF, width), BF)] * 2
    outs.append(jax.ShapeDtypeStruct((8, NT), F32))

    def piece(k):
        return pl.BlockSpec((1, S, C), lambda i: (k, 0, 0))

    def whole(v):
        return pl.BlockSpec(v.shape, lambda i: (0, 0))

    return pl.pallas_call(
        functools.partial(weight_grad_kernel, blocks, width),
        grid=(1,),
        in_specs=[piece(k) for k in blocks] + [whole(v) for v in acts],
        out_specs=[whole(v) for v in outs],
        out_shape=outs,
        compiler_params=params(24),
        cost_estimate=pl.CostEstimate(
            flops=2 * len(blocks) * S * C * width, bytes_accessed=9 << 20, transcendentals=0
        ),
        name="weight_grad",
    )(*([cols] * len(blocks)), *acts)


def far_start_kernel(cols_ref, own_ref, left_ref, right_ref, part_ref, peak_ref):
    peak_ref[...] = jnp.zeros_like(peak_ref)

    def step(i, carry):
        at = pl.ds(pl.multiple_of(i * NT, NT), NT)
        peak, total = peak_ref[...], None
        for j, ref in enumerate((own_ref, left_ref, right_ref)):
            part = jnp.dot(
                cols_ref[0, :, j * S : (j + 1) * S], ref[:, at], preferred_element_type=F32
            )
            peak = jnp.maximum(peak, jnp.max(jnp.abs(part).reshape(S // 8, 8, NT), axis=0))
            total = part if total is None else total + part
        part_ref[:, at] = total
        peak_ref[...] = peak
        return carry

    lax.fori_loop(0, C // NT, step, 0)


def far_finish_kernel(cols_ref, part_ref, top_ref, low_ref, peak_in, high_ref, low_out, peak_ref):
    peak_ref[...] = peak_in[...]

    def step(i, carry):
        at = pl.ds(pl.multiple_of(i * NT, NT), NT)
        right = jnp.concatenate([top_ref[:, at], low_ref[:, at]], axis=0)
        part = jnp.dot(cols_ref[0], right, preferred_element_type=F32)
        high = jnp.max(jnp.abs(part).reshape(S // 8, 8, NT), axis=0)
        peak_ref[...] = jnp.maximum(peak_ref[...], high)
        total = part_ref[:, at] + part
        high_ref[:, at] = total[:HALF].astype(BF)
        low_out[:, at] = total[HALF:].astype(BF)
        return carry

    lax.fori_loop(0, C // NT, step, 0)


def whole(shape):
    return pl.BlockSpec(shape, lambda i: (0,) * len(shape))


def weight_grad_far(cols, acts):
    small = jax.ShapeDtypeStruct((8, NT), F32)
    half = jax.ShapeDtypeStruct((HALF, C), BF)
    part, peak = pl.pallas_call(
        far_start_kernel,
        grid=(1,),
        in_specs=[whole((1, S, C))] + [whole((S, C))] * 3,
        out_specs=[whole((S, C)), whole((8, NT))],
        out_shape=[jax.ShapeDtypeStruct((S, C), F32), small],
        compiler_params=params(24),
        cost_estimate=pl.CostEstimate(
            flops=6 * S * S * C, bytes_accessed=6 << 20, transcendentals=0
        ),
        name="far_start",
    )(cols, *acts[:3])
    return pl.pallas_call(
        far_finish_kernel,
        grid=(1,),
        in_specs=[
            pl.BlockSpec((1, S, S), lambda i: (0, 0, 3)),
            whole((S, C)),
            whole((HALF, C)),
            whole((HALF, C)),
            whole((8, NT)),
        ],
        out_specs=[whole((HALF, C)), whole((HALF, C)), whole((8, NT))],
        out_shape=[half, half, small],
        compiler_params=params(24),
        cost_estimate=pl.CostEstimate(
            flops=2 * S * S * C, bytes_accessed=4 << 20, transcendentals=0
        ),
        name="far_finish",
    )(cols, part, acts[3], acts[4], peak)


STEP = 32


def fold_kernel(chunks, *refs):
    grad_ref, pair_ref = refs[-2:]
    peaks = refs[5 * len(chunks) : -2]

    squares = jnp.zeros((8, 128), F32)
    for k, (low, width) in enumerate(chunks):
        own, top_l, low_l, top_r, low_r = refs[5 * k : 5 * k + 5]

        def step(i, total, own=own, low=low, width=width, arms=((0, top_l, top_r), (HALF, low_l, low_r))):
            at = pl.multiple_of(i * STEP, STEP)
            for base, left, right in arms:
                rows = pl.ds(at, STEP)
                value = (
                    own[pl.ds(base + at, STEP), :]
                    + left[rows, :].astype(F32)
                    + right[rows, :].astype(F32)
                )
                grad_ref[pl.ds(base + at, STEP), low : low + width] = value
                square = (value * value).reshape(STEP // 8, 8, width).sum(axis=0)
                for j in range(width // 128):
                    total = total + square[:, j * 128 : (j + 1) * 128]
            return total

        squares = lax.fori_loop(0, HALF // STEP, step, squares)
    peak = peaks[0][...]
    for ref in peaks[1:]:
        peak = jnp.maximum(peak, ref[...])
    lane = lax.broadcasted_iota(jnp.int32, (128, 128), 1)
    pair_ref[...] = jnp.where(lane < 64, jnp.sum(squares), jnp.max(peak))


def fold_grad(parts, chunks, peaks):
    args = [v for part in parts for v in part] + list(peaks)
    return pl.pallas_call(
        functools.partial(fold_kernel, chunks),
        grid=(1,),
        in_specs=[pl.BlockSpec(v.shape, lambda i: (0, 0)) for v in args],
        out_specs=[
            pl.BlockSpec((S, C), lambda i: (0, 0)),
            pl.BlockSpec((128, 128), lambda i: (0, 0)),
        ],
        out_shape=[pltpu.HBM((S, C), F32), jax.ShapeDtypeStruct((128, 128), F32)],
        compiler_params=params(24),
        name="fold_grad",
    )(*args)


ROWS = 96


def adam_kernel(
    pairs_ref, grad_ref, moment_ref, second_ref, master_ref,
    moment_out, second_out, master_out, high_out, peak_out, again_ref, high_ref,
):
    i = pl.program_id(0)
    pairs = pairs_ref[...]
    squares = jnp.sum(pairs, axis=0, keepdims=True)[:, :1]
    clip_factor = jnp.minimum(1.0, jnp.sqrt(F32(OUT * IN)) / (jnp.sqrt(squares) + 1e-06))
    clipped = clip_factor * grad_ref[...]
    new_moment = 0.9 * moment_ref[...] + 0.1 * clipped
    new_second = 0.95 * second_ref[...] + 0.05 * clipped * clipped
    master = master_ref[...]
    new_master = master - 0.01 * (new_moment / (jnp.sqrt(new_second) + 1e-08) + 0.1 * master)
    moment_out[...] = new_moment
    second_out[...] = new_second
    master_out[...] = new_master
    again_ref[...] = new_master
    size = jnp.abs(new_master)
    high = size[:, :128]
    for j in range(1, C // 128):
        high = jnp.maximum(high, size[:, j * 128 : (j + 1) * 128])
    high_ref[pl.ds(pl.multiple_of(i * ROWS, ROWS), ROWS), :] = high

    @pl.when(i == S // ROWS - 1)
    def _():
        highs = jnp.max(high_ref[...].T, axis=0, keepdims=True)
        high_out[...] = jnp.broadcast_to(highs.reshape(1, 1, S), (8, 1, S))
        peak_out[...] = jnp.broadcast_to(jnp.max(pairs, axis=0, keepdims=True), (8, 128))


def adam(pairs, gradient, moment, second, master):
    block = pl.BlockSpec((ROWS, C), lambda i: (i, 0))
    small = jax.ShapeDtypeStruct((8, 128), F32)
    return pl.pallas_call(
        adam_kernel,
        grid=(S // ROWS,),
        in_specs=[pl.BlockSpec((128, 128), lambda i: (0, 0))] + [block] * 4,
        out_specs=[block] * 3
        + [whole((8, 1, S)), whole((8, 128)), block],
        out_shape=[jax.ShapeDtypeStruct((S, C), F32)] * 3
        + [jax.ShapeDtypeStruct((8, 1, S), F32), small, pltpu.VMEM((S, C), F32)],
        scratch_shapes=[pltpu.VMEM((S, 128), F32)],
        compiler_params=params(16),
        name="adam",
    )(pairs, gradient, moment, second, master)


def input_grad_kernel(count, own_last, *refs):
    rows, weights, outs = refs[:count], refs[count : count + 5], refs[count + 5 :]

    def step(i, carry):
        at = pl.ds(pl.multiple_of(i * NT, NT), NT)
        right = jnp.concatenate([w[:, at] for w in weights], axis=0)
        for k in range(count):
            total = jnp.dot(rows[k][0], right, preferred_element_type=F32)
            if own_last:
                outs[k][:, at] = total.astype(BF)
            else:
                outs[2 * k][:, at] = total[:HALF].astype(BF)
                outs[2 * k + 1][:, at] = total[HALF:].astype(BF)
        return carry

    lax.fori_loop(0, C // NT, step, 0)


def input_grad(rows, blocks, weights, own):
    half = jax.ShapeDtypeStruct((HALF, C), BF)
    outs = [pltpu.HBM((S, C), BF)] if own else [half] * (2 * len(blocks))

    def piece(k):
        return pl.BlockSpec((1, S, C), lambda i: (k, 0, 0))

    def whole(v):
        return pl.BlockSpec(v.shape, lambda i: (0, 0))

    return pl.pallas_call(
        functools.partial(input_grad_kernel, len(blocks), own),
        grid=(1,),
        in_specs=[piece(k) for k in blocks] + [whole(v) for v in weights],
        out_specs=[whole(v) for v in outs],
        out_shape=outs,
        compiler_params=params(24),
        cost_estimate=pl.CostEstimate(
            flops=2 * len(blocks) * S * C * C, bytes_accessed=9 << 20, transcendentals=0
        ),
        name="input_grad",
    )(*([rows] * len(blocks)), *weights)


def codes_kernel(highs_ref, master_ref, codes_ref, scales_ref):
    row_peak = jnp.max(highs_ref[...], axis=0) + 1e-06
    scales_ref[...] = row_peak
    column = jnp.broadcast_to(row_peak, (128, S)).T
    for j in range(C // 128):
        at = slice(j * 128, (j + 1) * 128)
        codes_ref[:, at] = (master_ref[:, at] / column).astype(BF)


def codes(highs, master):
    return pl.pallas_call(
        codes_kernel,
        grid=(1,),
        in_specs=[whole((8, 1, S)), whole((S, C))],
        out_specs=[whole((S, C)), whole((1, S))],
        out_shape=[jax.ShapeDtypeStruct((S, C), BF), jax.ShapeDtypeStruct((1, S), F32)],
        compiler_params=params(16),
        name="codes",
    )(highs, master)


def ring_gather(v, axis):
    left = shift(v, axis, 1)
    right = shift(v, axis, -1)
    top = shift(left[:HALF], axis, 1)
    bottom = shift(right[HALF:], axis, -1)
    return v, left, right, top, bottom


def ring_scatter(far, near, axis):
    up_a, up_b, down_a, down_b = near
    from_left = shift(far[0], axis, 1)
    from_right = shift(far[1], axis, -1)
    left_b = shift(up_b, axis, 1)
    right_a = shift(down_a, axis, -1)
    up_a = (up_a.astype(F32) + from_left.astype(F32)).astype(BF)
    down_b = (down_b.astype(F32) + from_right.astype(F32)).astype(BF)
    left_a = shift(up_a, axis, 1)
    right_b = shift(down_b, axis, -1)
    return left_a, left_b, right_a, right_b


CHUNKS = ((0, C),)


def step(inputs, out_grad, weight_codes, weight_scales, master, moment, second):
    to_up, to_down, to_far = split_grads(
        pltpu.with_memory_space_constraint(out_grad, pltpu.HBM)
    )
    mine = [shift(to_up, "x", 1), shift(to_down, "x", -1), shift(to_far, "x", 2)]
    mine = jnp.concatenate(mine, axis=0)
    acts = [ring_gather(inputs[:, low : low + width], "x") for low, width in CHUNKS]
    held = [mine] + [shift(mine, "y", s) for s in (1, -1, 2)]
    other = [shift(v, "c", 1) for v in held]
    rows, cols = assemble(out_grad, held + other)

    weight = (weight_codes.astype(F32) * weight_scales.astype(F32)[:, None]).astype(BF)
    ring = ring_gather(weight, "z")
    weights = (*ring[3:], ring[2], ring[1], ring[0])

    parts, peaks = [], []
    for act in acts:
        far_a, far_b, peak_a = weight_grad_far(cols, act)
        *near, own, peak_b = weight_grad(cols, (1, 2, 3), act)
        peaks += [peak_a, peak_b]
        parts.append((own, *ring_scatter((far_a, far_b), near, "z")))

    rows, _ = lax.optimization_barrier((rows, own))
    i_far = input_grad(rows, (3,), weights, False)
    i_near = input_grad(rows, (2, 1), weights, False)
    (i_own,) = input_grad(rows, (0,), weights, True)
    left_a, left_b, right_a, right_b = ring_scatter(i_far, i_near, "x")
    peaks, i_own = lax.optimization_barrier((peaks, i_own))
    top = i_own[:HALF].astype(F32) + left_a.astype(F32) + right_a.astype(F32)
    bottom = i_own[HALF:].astype(F32) + left_b.astype(F32) + right_b.astype(F32)
    grad_input = jnp.concatenate([top, bottom], axis=0).astype(BF)
    gradient, pair = fold_grad(parts, CHUNKS, peaks)
    pairs = lax.all_to_all(pair, ALL, 0, 0, tiled=True)
    gradient, moment, second, master = (
        pltpu.with_memory_space_constraint(v, pltpu.HBM)
        for v in (gradient, moment, second, master)
    )
    new_moment, new_second, new_master, high, peak, again = adam(
        pairs, gradient, moment, second, master
    )
    highs = lax.all_to_all(high, TENSOR, 0, 0, tiled=True)
    highs, grad_input = lax.optimization_barrier((highs, grad_input))
    new_codes, row_peak = codes(highs, pltpu.with_memory_space_constraint(again, pltpu.VMEM))
    new_scales = row_peak[0].astype(BF)
    return (grad_input, new_master, new_moment, new_second, new_codes, new_scales, peak[0, 64])


def solution(mesh):
    finer = Mesh(mesh.devices.reshape(4, 4, 4, 2), ALL)
    tiled = P(DP, TENSOR)
    in_specs = (tiled, P(DP, None), tiled, P(DP), tiled, tiled, tiled)
    out_specs = (tiled, tiled, tiled, tiled, tiled, P(DP), P())
    return jax.shard_map(step, mesh=finer, in_specs=in_specs, out_specs=out_specs, check_vma=False)
```
